32 devices in a mesh: order: 4 (over z), degree: 2 (over y), site: 4 (over x, core).
Axes of the slice: x: 2, y: 2, z: 4, core: 2. Of those that a mesh axis runs over, the one named last changes fastest.
Arguments:
- scene_coeffs: bfloat16 [2, 16, 128, 256, 32], P(None, None, 'degree', 'order'), may hold values from -3 to 3
- site_ids: int32 [4], P('site'), may hold values from 0 to 31
- gripper_coeffs: bfloat16 [2, 16, 128, 256], P(None, None, 'degree', 'order'), may hold values from -3 to 3
- order_table: int32 [256], replicated, may hold values from 0 to 255, each once
- wigner: bfloat16 [128, 8, 256, 256], P('degree', None, 'order'), may hold values from -0.0029907227 to 0.0029907227
Outputs:
- scores: float32 [4, 8, 256, 256], P('site', 'degree', 'order')
The draws below stay inside these ranges and needn't reach their ends.
Inputs may be any that keep to these rules, and one draw needn't show every extreme that they name: A permutation of the 256 slots; slot j holds order order_table[j] - 128. `site_ids`: sites may share a candidate.
All inputs are finite; a program needn't handle non-finite values.
Results may differ from the reference program's by a relative error of at most 0.0029.
Values may be sent and summed in bfloat16 or wider, within the bound.
A program may use at most 128 MiB of HBM per device.

```python
import math
import jax
import jax.numpy as jnp
from jax import lax

B = 128
C = 16
CAND = 32
NB = 8
SITES = 4
SLOTS = 256
GRID = 256


def touch_ends(result, own_key, least, largest):
    shape = result.shape
    spot = [jax.random.randint(jax.random.fold_in(own_key, axis), (), 0, shape[axis]) for axis in range(len(shape))]
    result = result.at[tuple(spot)].set(least)
    longest = shape.index(max(shape))
    spot[longest] = (spot[longest] + 1) % shape[longest]
    return result.at[tuple(spot)].set(largest)


def level_of(key, shape, cuts, low, high):
    gain, own = 1.0, jax.random.fold_in(key, 6)
    for position, blocks in cuts:
        heights = jnp.exp(jax.random.uniform(jax.random.fold_in(own, position), (blocks,), jnp.float32, low / len(cuts), high / len(cuts)))
        gain = gain * jnp.repeat(heights, shape[position] // blocks).reshape([-1 if axis == position else 1 for axis in range(len(shape))])
    return gain


def scatter_about(rng, dims, spread, limit, pieces=(), held_as=jnp.bfloat16):
    gain = level_of(rng, dims, pieces, -0.22, 0.18) if pieces else 1.0
    array = jax.random.normal(rng, dims, jnp.float32) * spread * gain
    return jnp.minimum(jnp.maximum(array, -limit), limit).astype(held_as)


def setup_inputs(seed: int = 0) -> dict:
    splits = jax.random.split(jax.random.key(seed), 6)
    return {
        "scene_coeffs": scatter_about(splits[0], (2, C, B, SLOTS, CAND), 0.5, 3.0, ((2, 2), (3, 4))),
        "site_ids": touch_ends(jax.random.randint(splits[1], (SITES,), 0, CAND), jax.random.fold_in(splits[1], 1), 0, CAND - 1).astype(jnp.int32),
        "gripper_coeffs": scatter_about(splits[2], (2, C, B, SLOTS), 0.5, 3.0, ((2, 2), (3, 4))),
        "order_table": jax.random.permutation(splits[3], SLOTS).astype(jnp.int32),
        "wigner": scatter_about(splits[4], (B, NB, SLOTS, SLOTS), 0.0005, 0.0029907227, ((0, 2), (2, 4))),
    }


def phase_tables(order_table):
    orders = order_table.astype(jnp.int32) - B
    angles = jnp.arange(GRID, dtype=jnp.int32)
    phase_index = jnp.mod(orders[:, None] * angles[None, :], GRID)
    radians = phase_index.astype(jnp.float32) * (2.0 * math.pi / GRID)
    return orders, jnp.cos(radians), jnp.sin(radians)


def reference(scene_coeffs, site_ids, gripper_coeffs, order_table, wigner):
    orders, cosine, sine_table = phase_tables(order_table)
    magnitude = jnp.abs(orders)
    chosen = jnp.take(scene_coeffs, site_ids.astype(jnp.int32), axis=4).astype(jnp.float32)
    gripper = gripper_coeffs.astype(jnp.float32)

    def one_degree(carried, inputs):
        scene_part, grip_part, wigner_part, degree = inputs
        real_part = jnp.einsum("cms,cp->spm", scene_part[0], grip_part[0]) + jnp.einsum("cms,cp->spm", scene_part[1], grip_part[1])
        imag_part = jnp.einsum("cms,cp->spm", scene_part[1], grip_part[0]) - jnp.einsum("cms,cp->spm", scene_part[0], grip_part[1])
        permitted_mask = (magnitude[:, None] <= degree) & (magnitude[None, :] <= degree)
        product = jnp.where(permitted_mask[None, None], jnp.stack([real_part, imag_part]), jnp.float32(0.0))
        product = lax.optimization_barrier(product.astype(jnp.bfloat16)).astype(jnp.float32)
        weights = wigner_part.astype(jnp.float32)
        return carried + jnp.einsum("xspm,bpm->xsbpm", product, weights), None

    initial = jnp.zeros((2, SITES, NB, SLOTS, SLOTS), jnp.float32)
    inputs = (jnp.moveaxis(chosen, 2, 0), jnp.moveaxis(gripper, 2, 0), wigner, jnp.arange(B, dtype=jnp.int32))
    summed, _ = lax.scan(one_degree, initial, inputs)
    highest = lax.Precision.HIGHEST
    real_alpha = jnp.einsum("sbpm,mj->sbpj", summed[0], cosine, precision=highest) - jnp.einsum("sbpm,mj->sbpj", summed[1], sine_table, precision=highest)
    imag_alpha = jnp.einsum("sbpm,mj->sbpj", summed[0], sine_table, precision=highest) + jnp.einsum("sbpm,mj->sbpj", summed[1], cosine, precision=highest)
    scores = jnp.einsum("sbpj,pk->sbjk", real_alpha, cosine, precision=highest) - jnp.einsum("sbpj,pk->sbjk", imag_alpha, sine_table, precision=highest)
    return scores
```

```python
import math

import jax
import jax.numpy as jnp
from jax import lax
from jax.experimental import pallas as pl
from jax.experimental.pallas import tpu as pltpu
from jax.sharding import PartitionSpec as P


def general_shards(scene_coeffs, site_ids, gripper_coeffs, order_table, wigner):
    highest = lax.Precision.HIGHEST
    slot_count = order_table.shape[0]
    local_deg = gripper_coeffs.shape[2]
    local_ord = gripper_coeffs.shape[3]
    cand_count = scene_coeffs.shape[4]
    site_count = site_ids.shape[0]
    order_pos = lax.axis_index("order")
    degree_pos = lax.axis_index("degree")
    orders = order_table - slot_count // 2
    angles = jnp.arange(slot_count, dtype=jnp.int32)
    phase_index = jnp.mod(orders[:, None] * angles[None, :], slot_count)
    radians = phase_index.astype(jnp.float32) * (2.0 * math.pi / slot_count)
    cosine = jnp.cos(radians)
    sine_table = jnp.sin(radians)
    magnitude = jnp.abs(orders)
    resident_degrees = degree_pos * local_deg + jnp.arange(local_deg, dtype=jnp.int32)
    owned_orders = lax.dynamic_slice_in_dim(magnitude, order_pos * local_ord, local_ord)
    grip_allowed = owned_orders[None, :] <= resident_degrees[:, None]
    selector = (jnp.arange(cand_count, dtype=jnp.int32)[:, None] == site_ids[None, :]).astype(
        jnp.bfloat16
    )
    chosen = jnp.dot(
        scene_coeffs.reshape(-1, cand_count), selector, preferred_element_type=jnp.float32
    )
    chosen = chosen.astype(jnp.bfloat16).reshape(
        2, scene_coeffs.shape[1], local_deg, local_ord, site_count
    )
    grip_real = jnp.concatenate([gripper_coeffs[0], gripper_coeffs[1]], axis=0)
    grip_imag = jnp.concatenate([-gripper_coeffs[1], gripper_coeffs[0]], axis=0)
    gripper_couple = jnp.stack([grip_real, grip_imag])
    columns_in = lax.all_gather(chosen, "order", axis=3, tiled=True)
    scene_joined = jnp.concatenate([columns_in[0], columns_in[1]], axis=0)
    product = jnp.einsum(
        "aonw,iaob->iobnw", scene_joined, gripper_couple, preferred_element_type=jnp.float32
    )
    permitted_mask = grip_allowed[:, :, None] & (
        magnitude[None, None, :] <= resident_degrees[:, None, None]
    )
    product = jnp.where(permitted_mask[None, :, :, :, None], product, jnp.float32(0.0)).astype(
        jnp.bfloat16
    )
    partial_value = jnp.einsum(
        "ylprs,lbpr->ysbpr", product, wigner, preferred_element_type=jnp.float32
    )
    summed = lax.psum_scatter(partial_value, "degree", scatter_dimension=2, tiled=True)
    phase_pair = jnp.concatenate([cosine, sine_table], axis=1)
    products = jnp.einsum(
        "xsbpm,mk->xsbpk", summed, phase_pair, precision=highest, preferred_element_type=jnp.float32
    )
    real_alpha = products[0, ..., :slot_count] - products[1, ..., slot_count:]
    imag_alpha = products[0, ..., slot_count:] + products[1, ..., :slot_count]
    stacked_parts = jnp.stack([real_alpha, imag_alpha])
    exchanged = lax.all_to_all(stacked_parts, "order", split_axis=4, concat_axis=3, tiled=True)
    first_term = jnp.einsum(
        "sbpa,pk->sbak", exchanged[0], cosine, precision=highest, preferred_element_type=jnp.float32
    )
    latter_addend = jnp.einsum(
        "sbpa,pk->sbak",
        exchanged[1],
        sine_table,
        precision=highest,
        preferred_element_type=jnp.float32,
    )
    return first_term - latter_addend


MESH = pl.DeviceIdType.MESH
F32, BF16 = jnp.float32, jnp.bfloat16
CHUNKS = 4


def cos_of(index, count):
    centred = jnp.bitwise_and(index + count // 2, count - 1) - count // 2
    half = centred.astype(F32) * F32(math.pi / count)
    sq = half * half
    poly = F32(-1.0 / 39916800.0)
    for coefficient in (1.0 / 362880.0, -1.0 / 5040.0, 1.0 / 120.0, -1.0 / 6.0, 1.0):
        poly = poly * sq + F32(coefficient)
    sine = poly * half
    return 1.0 - 2.0 * sine * sine


def split(value):
    high = value.astype(BF16)
    return high, (value - high.astype(F32)).astype(BF16)


def fused_kernel(
    s_ref, g_ref, col_ref, row_ref, w_ref, out_ref,
    wbuf, sbuf, prod, accbuf, rs_send, rs_recv, a_send, a_recv, halfacc,
    alpha_hi, alpha_lo, gamma_hi, gamma_lo,
    w_sem, s_send_sem, s_recv_sem, r_send_sem, r_recv_sem, x_send_sem, x_recv_sem,
):
    me = lax.axis_index("order")
    deg = lax.axis_index("degree")
    L, NBETA, P, M = wbuf.shape[1:]
    SL = 2 * M
    BO = NBETA // 2
    first = me // 2
    second = 1 - first
    per = L // CHUNKS

    def w_copy(h, c):
        return pltpu.make_async_copy(
            w_ref.at[pl.ds(c * per, per), :, :, pl.ds(pl.multiple_of(h * M, M), M)],
            wbuf.at[h, pl.ds(c * per, per)],
            w_sem.at[h, c],
        )

    for h in (first, second):
        for c in range(CHUNKS):
            w_copy(h, c).start()

    barrier = pltpu.get_barrier_semaphore()
    for off in (1, 2, 3):
        pl.semaphore_signal(barrier, 1, device_id={"order": (me + off) % 4}, device_id_type=MESH)
    pl.semaphore_signal(barrier, 1, device_id={"degree": 1 - deg}, device_id_type=MESH)
    pl.semaphore_wait(barrier, 4)

    def s_copy(target, slot, off):
        return pltpu.make_async_remote_copy(
            src_ref=s_ref, dst_ref=sbuf.at[slot],
            send_sem=s_send_sem.at[off], recv_sem=s_recv_sem.at[off],
            device_id={"order": target}, device_id_type=MESH,
        )

    for off in (1, 3, 2):
        s_copy((me + off) % 4, me, off).start()

    def s_wait(source):
        off = (me - source + 4) % 4
        s_copy(source, source, off).wait_recv()

    sbuf[me] = s_ref[...]

    ang = lax.broadcasted_iota(jnp.int32, (M, 2 * SL), 1)
    tgt = (ang // 128) * P + ang % P
    part = (ang // P) % 2
    quarter = SL // 4
    for h in range(2):
        orders = col_ref[h * M : (h + 1) * M, :] - SL // 2
        for x in range(2):
            table = cos_of(orders * tgt + (x - part) * quarter, SL)
            hi, lo = split(table)
            alpha_hi[h, x * M : (x + 1) * M, :] = hi
            alpha_lo[h, x * M : (x + 1) * M, :] = lo
        table = cos_of(orders * (ang % SL) + (ang // SL) * quarter, SL)
        hi, lo = split(table)
        gamma_hi[h * M : (h + 1) * M, :] = hi
        gamma_lo[h * M : (h + 1) * M, :] = lo

    mag_p = jnp.abs(col_ref[pl.ds(pl.multiple_of(me * P, P), P), :] - SL // 2)
    dims = (((0,), (0,)), ((), ()))

    def compute(h):
        mag_m = jnp.abs(row_ref[h] - SL // 2)
        most = jnp.maximum(jnp.broadcast_to(mag_p, (P, M)), jnp.broadcast_to(mag_m, (P, M)))
        most = jnp.concatenate([most, most], axis=0)

        def product(step, carry):
            b0, b1 = sbuf[2 * h, step], sbuf[2 * h + 1, step]
            low = jnp.concatenate([b0[:, :P], b1[:, :P]], axis=1)
            high = jnp.concatenate([b0[:, P:], b1[:, P:]], axis=1)
            for l, scene in ((step, low), (step + L // 2, high)):
                value = lax.dot_general(g_ref[l], scene, dims, preferred_element_type=F32)
                value = jnp.where(most <= deg * L + l, value, F32(0.0))
                prod[l] = value.astype(BF16)
            return carry

        lax.fori_loop(0, L // 2, product, 0)
        for c in range(CHUNKS):
            w_copy(h, c).wait()

        ROWS = 16

        def rows(blk, carry):
            at = pl.multiple_of(blk * ROWS, ROWS)

            def degree_step(l, acc):
                pr = prod[l, pl.ds(at, ROWS), :].astype(F32)
                pi = prod[l, pl.ds(at + P, ROWS), :].astype(F32)
                new = []
                for b in range(NBETA):
                    w = wbuf[h, l, b, pl.ds(at, ROWS), :].astype(F32)
                    new.append(acc[2 * b] + pr * w)
                    new.append(acc[2 * b + 1] + pi * w)
                return tuple(new)

            zero = jnp.zeros((ROWS, M), F32)
            acc = lax.fori_loop(0, L, degree_step, (zero,) * (2 * NBETA), unroll=2)
            for b in range(NBETA):
                accbuf[h, b, 0, pl.ds(at, ROWS), :] = acc[2 * b]
                accbuf[h, b, 1, pl.ds(at, ROWS), :] = acc[2 * b + 1]
            return carry

        lax.fori_loop(0, P // ROWS, rows, 0)
        rs_send[h] = accbuf[h, pl.ds((1 - deg) * BO, BO)].astype(BF16)

    def r_copy(h):
        return pltpu.make_async_remote_copy(
            src_ref=rs_send.at[h], dst_ref=rs_recv.at[h],
            send_sem=r_send_sem.at[h], recv_sem=r_recv_sem.at[h],
            device_id={"degree": 1 - deg}, device_id_type=MESH,
        )

    def alpha(h):
        r_copy(h).wait_recv()
        total = accbuf[h, pl.ds(deg * BO, BO)] + rs_recv[h].astype(F32)
        total = jnp.concatenate(
            [total[:, 0].reshape(BO * P, M), total[:, 1].reshape(BO * P, M)], axis=1
        )
        hi, lo = split(total)
        value = jnp.dot(hi, alpha_hi[h], preferred_element_type=F32)
        value += jnp.dot(hi, alpha_lo[h], preferred_element_type=F32)
        value += jnp.dot(lo, alpha_hi[h], preferred_element_type=F32)
        return value

    s_wait(first * 2 + (1 - me % 2))
    compute(first)
    r_copy(first).start()
    s_wait(second * 2 + (1 - first))
    s_wait(second * 2 + first)
    compute(second)
    r_copy(second).start()
    halfacc[...] = alpha(first)
    value = (halfacc[...] + alpha(second)).astype(BF16)
    for t in range(4):
        a_send[t] = value[:, t * 128 : (t + 1) * 128]

    def x_copy(target, source, off):
        return pltpu.make_async_remote_copy(
            src_ref=a_send.at[target], dst_ref=a_recv.at[source],
            send_sem=x_send_sem.at[off], recv_sem=x_recv_sem.at[off],
            device_id={"order": target}, device_id_type=MESH,
        )

    for off in (2, 1, 3):
        x_copy((me + off) % 4, me, off).start()
    a_recv[me] = a_send[me]
    for off in (1, 3, 2):
        source = (me - off + 4) % 4
        x_copy(source, source, off).wait_recv()

    for b in range(BO):
        got = jnp.concatenate([a_recv[z, b * P : (b + 1) * P, :] for z in range(4)], axis=0)
        score = jnp.zeros((P, SL), F32)
        for x in range(2):
            for table in (gamma_hi, gamma_lo):
                score += lax.dot_general(
                    got[:, x * P : (x + 1) * P], table[:, x * SL : (x + 1) * SL], dims,
                    preferred_element_type=F32,
                )
        out_ref[0, b] = score

    for off in (1, 2, 3):
        s_copy((me + off) % 4, me, off).wait_send()
        x_copy((me + off) % 4, me, off).wait_send()
    r_copy(first).wait_send()
    r_copy(second).wait_send()


def fused_shards(scene_coeffs, site_ids, gripper_coeffs, order_table, wigner):
    L, NBETA, P, SL = wigner.shape
    M = SL // 2
    K = 2 * scene_coeffs.shape[1]
    chosen = lax.dynamic_index_in_dim(scene_coeffs, site_ids[0], axis=4, keepdims=False)
    s = jnp.transpose(chosen, (2, 0, 1, 3)).reshape(2, L // 2, K, P)
    s = jnp.concatenate([s[0], s[1]], axis=-1)
    couple = jnp.concatenate(
        [gripper_coeffs, jnp.stack([-gripper_coeffs[1], gripper_coeffs[0]])], axis=-1
    )
    g = jnp.transpose(couple, (2, 0, 1, 3)).reshape(L, K, 2 * P)
    vmem = pl.BlockSpec(memory_space=pltpu.VMEM)
    BO = NBETA // 2
    return pl.pallas_call(
        fused_kernel,
        out_shape=jax.ShapeDtypeStruct((1, BO, P, SL), F32),
        in_specs=[vmem, vmem, vmem, vmem, pl.BlockSpec(memory_space=pl.ANY)],
        out_specs=vmem,
        scratch_shapes=[
            pltpu.VMEM((2, L, NBETA, P, M), BF16),
            pltpu.VMEM((4, L // 2, K, 2 * P), BF16),
            pltpu.VMEM((L, 2 * P, M), BF16),
            pltpu.VMEM((2, NBETA, 2, P, M), F32),
            pltpu.VMEM((2, BO, 2, P, M), BF16),
            pltpu.VMEM((2, BO, 2, P, M), BF16),
            pltpu.VMEM((4, BO * P, 128), BF16),
            pltpu.VMEM((4, BO * P, 128), BF16),
            pltpu.VMEM((BO * P, 2 * SL), F32),
            pltpu.VMEM((2, 2 * M, 2 * SL), BF16),
            pltpu.VMEM((2, 2 * M, 2 * SL), BF16),
            pltpu.VMEM((SL, 2 * SL), BF16),
            pltpu.VMEM((SL, 2 * SL), BF16),
            pltpu.SemaphoreType.DMA((2, CHUNKS)),
            pltpu.SemaphoreType.DMA((4,)),
            pltpu.SemaphoreType.DMA((4,)),
            pltpu.SemaphoreType.DMA((2,)),
            pltpu.SemaphoreType.DMA((2,)),
            pltpu.SemaphoreType.DMA((4,)),
            pltpu.SemaphoreType.DMA((4,)),
        ],
        compiler_params=pltpu.CompilerParams(
            collective_id=0, has_side_effects=True, vmem_limit_bytes=48 * 1024 * 1024
        ),
    )(s, g, order_table.reshape(SL, 1), order_table.reshape(2, 1, M), wigner)


def solution(mesh):
    fits = mesh.shape["order"] == 4 and mesh.shape["degree"] == 2 and mesh.shape["site"] == 4
    shards = fused_shards if fits else general_shards
    in_specs = (
        P(None, None, "degree", "order", None),
        P("site"),
        P(None, None, "degree", "order"),
        P(),
        P("degree", None, "order", None),
    )
    out_specs = P("site", "degree", "order", None)
    return jax.shard_map(shards, mesh=mesh, in_specs=in_specs, out_specs=out_specs, check_vma=False)
```

```python
import math

import jax
import jax.numpy as jnp
from jax import lax
from jax.experimental import pallas as pl
from jax.experimental.pallas import tpu as pltpu
from jax.sharding import PartitionSpec as P


def general_shards(scene_coeffs, site_ids, gripper_coeffs, order_table, wigner):
    highest = lax.Precision.HIGHEST
    slot_count = order_table.shape[0]
    local_deg = gripper_coeffs.shape[2]
    local_ord = gripper_coeffs.shape[3]
    cand_count = scene_coeffs.shape[4]
    site_count = site_ids.shape[0]
    order_pos = lax.axis_index("order")
    degree_pos = lax.axis_index("degree")
    orders = order_table - slot_count // 2
    angles = jnp.arange(slot_count, dtype=jnp.int32)
    phase_index = jnp.mod(orders[:, None] * angles[None, :], slot_count)
    radians = phase_index.astype(jnp.float32) * (2.0 * math.pi / slot_count)
    cosine = jnp.cos(radians)
    sine_table = jnp.sin(radians)
    magnitude = jnp.abs(orders)
    resident_degrees = degree_pos * local_deg + jnp.arange(local_deg, dtype=jnp.int32)
    owned_orders = lax.dynamic_slice_in_dim(magnitude, order_pos * local_ord, local_ord)
    grip_allowed = owned_orders[None, :] <= resident_degrees[:, None]
    selector = (jnp.arange(cand_count, dtype=jnp.int32)[:, None] == site_ids[None, :]).astype(
        jnp.bfloat16
    )
    chosen = jnp.dot(
        scene_coeffs.reshape(-1, cand_count), selector, preferred_element_type=jnp.float32
    )
    chosen = chosen.astype(jnp.bfloat16).reshape(
        2, scene_coeffs.shape[1], local_deg, local_ord, site_count
    )
    grip_real = jnp.concatenate([gripper_coeffs[0], gripper_coeffs[1]], axis=0)
    grip_imag = jnp.concatenate([-gripper_coeffs[1], gripper_coeffs[0]], axis=0)
    gripper_couple = jnp.stack([grip_real, grip_imag])
    columns_in = lax.all_gather(chosen, "order", axis=3, tiled=True)
    scene_joined = jnp.concatenate([columns_in[0], columns_in[1]], axis=0)
    product = jnp.einsum(
        "aonw,iaob->iobnw", scene_joined, gripper_couple, preferred_element_type=jnp.float32
    )
    permitted_mask = grip_allowed[:, :, None] & (
        magnitude[None, None, :] <= resident_degrees[:, None, None]
    )
    product = jnp.where(permitted_mask[None, :, :, :, None], product, jnp.float32(0.0)).astype(
        jnp.bfloat16
    )
    partial_value = jnp.einsum(
        "ylprs,lbpr->ysbpr", product, wigner, preferred_element_type=jnp.float32
    )
    summed = lax.psum_scatter(partial_value, "degree", scatter_dimension=2, tiled=True)
    phase_pair = jnp.concatenate([cosine, sine_table], axis=1)
    products = jnp.einsum(
        "xsbpm,mk->xsbpk", summed, phase_pair, precision=highest, preferred_element_type=jnp.float32
    )
    real_alpha = products[0, ..., :slot_count] - products[1, ..., slot_count:]
    imag_alpha = products[0, ..., slot_count:] + products[1, ..., :slot_count]
    stacked_parts = jnp.stack([real_alpha, imag_alpha])
    exchanged = lax.all_to_all(stacked_parts, "order", split_axis=4, concat_axis=3, tiled=True)
    first_term = jnp.einsum(
        "sbpa,pk->sbak", exchanged[0], cosine, precision=highest, preferred_element_type=jnp.float32
    )
    latter_addend = jnp.einsum(
        "sbpa,pk->sbak",
        exchanged[1],
        sine_table,
        precision=highest,
        preferred_element_type=jnp.float32,
    )
    return first_term - latter_addend


MESH = pl.DeviceIdType.MESH
F32, BF16 = jnp.float32, jnp.bfloat16
CHUNKS = 4
ROWS = 16


def cos_of(index, count):
    centred = jnp.bitwise_and(index + count // 2, count - 1) - count // 2
    half = centred.astype(F32) * F32(math.pi / count)
    sq = half * half
    poly = F32(-1.0 / 39916800.0)
    for coefficient in (1.0 / 362880.0, -1.0 / 5040.0, 1.0 / 120.0, -1.0 / 6.0, 1.0):
        poly = poly * sq + F32(coefficient)
    sine = poly * half
    return 1.0 - 2.0 * sine * sine


def split(value):
    high = value.astype(BF16)
    return high, (value - high.astype(F32)).astype(BF16)


def fused_kernel(
    s_ref, g_ref, row_ref, w_ref, out_ref,
    wbuf, sbuf, prod, accbuf, rs_send, rs_recv, a_send, a_recv, halfacc,
    alpha_hi, alpha_lo, gamma_hi, gamma_lo, g32, col,
    w_sem, s_send_sem, s_recv_sem, r_send_sem, r_recv_sem, x_send_sem, x_recv_sem,
):
    me = lax.axis_index("order")
    deg = lax.axis_index("degree")
    HL, NBETA, P, M = wbuf.shape[2:]
    L = 2 * HL
    SL = 2 * M
    BO = NBETA // 2
    K = s_ref.shape[1]
    first = me // 2
    second = 1 - first
    near = first * 2 + (1 - me % 2)
    per = HL // CHUNKS
    blocks = P // ROWS

    def w_copy(h, c):
        return pltpu.make_async_copy(
            w_ref.at[:, pl.ds(c * per, per), :, :, pl.ds(pl.multiple_of(h * M, M), M)],
            wbuf.at[h, :, pl.ds(c * per, per)],
            w_sem.at[h, c],
        )

    barrier = pltpu.get_barrier_semaphore()
    for off in (1, 2, 3):
        pl.semaphore_signal(barrier, 1, device_id={"order": (me + off) % 4}, device_id_type=MESH)
    pl.semaphore_signal(barrier, 1, device_id={"degree": 1 - deg}, device_id_type=MESH)

    for h in (first, second):
        for c in range(CHUNKS):
            w_copy(h, c).start()

    pl.semaphore_wait(barrier, 4)

    def hop(block, c, way, own=False):
        rows = pl.ds(c * per, per)
        return pltpu.make_async_remote_copy(
            src_ref=s_ref.at[rows] if own else sbuf.at[block, rows],
            dst_ref=sbuf.at[block, rows],
            send_sem=s_send_sem.at[way, block, c], recv_sem=s_recv_sem.at[block, c],
            device_id={"order": me + 1 - 2 * way}, device_id_type=MESH,
        )

    for c in range(CHUNKS):
        @pl.when(me < 3)
        def _():
            hop(me, c, 0, True).start()

        @pl.when(me > 0)
        def _():
            hop(me, c, 1, True).start()

    sbuf[me] = s_ref[...]

    for h in range(2):
        line = jnp.broadcast_to(row_ref[h].astype(F32), (M, M))
        col[h * M : (h + 1) * M, :] = jnp.transpose(line).astype(jnp.int32) - SL // 2
    real = g_ref[0].astype(F32).reshape(K // 2 * L, P)
    imag = g_ref[1].astype(F32).reshape(K // 2 * L, P)
    g32[: K // 2 * L] = jnp.concatenate([real, -imag], axis=1)
    g32[K // 2 * L :] = jnp.concatenate([imag, real], axis=1)
    accbuf[...] = jnp.zeros_like(accbuf)
    mag_p = jnp.abs(col[pl.ds(pl.multiple_of(me * P, P), P), :])
    dims = (((0,), (0,)), ((), ()))

    def tables():
        quarter = SL // 4
        lane = lax.broadcasted_iota(jnp.int32, (M, M), 1)
        for h in range(2):
            orders = col[h * M : (h + 1) * M, :]
            for t in range(4):
                at = slice(t * M, (t + 1) * M)
                phase = orders * (t * P + lane % P)
                for x in range(2):
                    hi, lo = split(cos_of(phase + (x - lane // P) * quarter, SL))
                    alpha_hi[h, x * M : (x + 1) * M, at] = hi
                    alpha_lo[h, x * M : (x + 1) * M, at] = lo
                phase = orders * ((t % 2) * M + lane)
                hi, lo = split(cos_of(phase + (t // 2) * quarter, SL))
                gamma_hi[h * M : (h + 1) * M, at] = hi
                gamma_lo[h * M : (h + 1) * M, at] = lo

    def r_copy(h, blk):
        return pltpu.make_async_remote_copy(
            src_ref=rs_send.at[h, blk], dst_ref=rs_recv.at[h, blk],
            send_sem=r_send_sem.at[h, blk], recv_sem=r_recv_sem.at[h, blk],
            device_id={"degree": 1 - deg}, device_id_type=MESH,
        )

    def compute(h, arrivals):
        mag_m = jnp.abs(row_ref[h] - SL // 2)
        most = jnp.maximum(mag_p, jnp.broadcast_to(mag_m, (P, M)))
        most = jnp.concatenate([most, most], axis=0)

        def chunk(c, carry):
            arrivals(c)
            for i in range(per):
                step = c * per + i
                b0, b1 = sbuf[2 * h, step], sbuf[2 * h + 1, step]
                low = jnp.concatenate([b0[:, :P], b1[:, :P]], axis=1)
                high = jnp.concatenate([b0[:, P:], b1[:, P:]], axis=1)
                for part, scene in ((0, low), (1, high)):
                    l = step + part * HL
                    grip = g32[pl.ds(l, K, stride=L), :].astype(BF16)
                    value = lax.dot_general(grip, scene, dims, preferred_element_type=F32)
                    value = jnp.where(most <= deg * L + l, value, F32(0.0))
                    prod[part, i] = value.astype(BF16)
            w_copy(h, c).wait()

            def rows(blk, carry):
                at = pl.multiple_of(blk * ROWS, ROWS)

                def degree_step(i, acc):
                    acc = list(acc)
                    for part in range(2):
                        pr = prod[part, i, pl.ds(at, ROWS), :].astype(F32)
                        pi = prod[part, i, pl.ds(at + P, ROWS), :].astype(F32)
                        for b in range(NBETA):
                            w = wbuf[h, part, c * per + i, b, pl.ds(at, ROWS), :].astype(F32)
                            acc[2 * b] += pr * w
                            acc[2 * b + 1] += pi * w
                    return tuple(acc)

                acc = tuple(accbuf[h, blk, n // 2, n % 2] for n in range(2 * NBETA))
                acc = lax.fori_loop(0, per, degree_step, acc, unroll=2)
                for n in range(2 * NBETA):
                    accbuf[h, blk, n // 2, n % 2] = acc[n]

                @pl.when(c == CHUNKS - 1)
                def _():
                    rs_send[h, blk] = accbuf[h, blk, pl.ds((1 - deg) * BO, BO)].astype(BF16)
                    r_copy(h, blk).start()

                return carry

            return lax.fori_loop(0, blocks, rows, carry)

        lax.fori_loop(0, CHUNKS, chunk, 0)

    def alpha(h, blk):
        r_copy(h, blk).wait_recv()
        total = accbuf[h, blk, pl.ds(deg * BO, BO)] + rs_recv[h, blk].astype(F32)
        total = jnp.concatenate(
            [total[:, 0].reshape(BO * ROWS, M), total[:, 1].reshape(BO * ROWS, M)], axis=1
        )
        hi, lo = split(total)
        value = jnp.dot(hi, alpha_hi[h], preferred_element_type=F32)
        value += jnp.dot(hi, alpha_lo[h], preferred_element_type=F32)
        value += jnp.dot(lo, alpha_hi[h], preferred_element_type=F32)
        return value

    across = lax.max(me - 1, 0) % 2
    middle = (me == 1) | (me == 2)
    other = me + 1 - 2 * across
    beyond = other + 1 - 2 * across

    def wait_block(block, c):
        hop(block, c, me // 3).wait_recv()

    def arrivals_first(c):
        wait_block(near, c)

        @pl.when(middle)
        def _():
            hop(near, c, across).start()
            wait_block(other, c)
            hop(other, c, 1 - across).start()

    def arrivals_second(c):
        @pl.when(middle)
        def _():
            wait_block(beyond, c)
            hop(beyond, c, 1 - across).start()

        @pl.when(jnp.logical_not(middle))
        def _():
            wait_block(second * 2, c)
            wait_block(second * 2 + 1, c)

    tables()
    compute(first, arrivals_first)
    compute(second, arrivals_second)

    def x_copy(target, source, blk, off):
        return pltpu.make_async_remote_copy(
            src_ref=a_send.at[target, blk], dst_ref=a_recv.at[source, blk],
            send_sem=x_send_sem.at[off, blk], recv_sem=x_recv_sem.at[off, blk],
            device_id={"order": target}, device_id_type=MESH,
        )

    for blk in range(blocks):
        halfacc[blk] = alpha(first, blk)
    for blk in range(blocks):
        value = (halfacc[blk] + alpha(second, blk)).astype(BF16)
        for t in range(4):
            a_send[t, blk] = value[:, t * M : (t + 1) * M]
        for off in (2, 1, 3):
            x_copy((me + off) % 4, me, blk, off).start()
        a_recv[me, blk] = a_send[me, blk]

    for blk in range(blocks):
        for off in (1, 3, 2):
            source = (me - off + 4) % 4
            x_copy(source, source, blk, off).wait_recv()

    score = jnp.zeros((BO * P, SL), F32)
    got = [
        jnp.concatenate(
            [a_recv[z, blk, b * ROWS : (b + 1) * ROWS, :] for z in range(4) for blk in range(blocks)],
            axis=0,
        )
        for b in range(BO)
    ]
    for x in range(2):
        left = jnp.concatenate([piece[:, x * P : (x + 1) * P] for piece in got], axis=1)
        for table in (gamma_hi, gamma_lo):
            score += lax.dot_general(
                left, table[:, x * SL : (x + 1) * SL], dims, preferred_element_type=F32
            )
    out_ref[0] = score.reshape(BO, P, SL)

    for c in range(CHUNKS):
        @pl.when(me < 3)
        def _():
            hop(me, c, 0, True).wait_send()

        @pl.when(me > 0)
        def _():
            hop(me, c, 1, True).wait_send()

        @pl.when(middle)
        def _():
            hop(near, c, across).wait_send()
            hop(other, c, 1 - across).wait_send()
            hop(beyond, c, 1 - across).wait_send()

    for blk in range(blocks):
        for off in (1, 2, 3):
            x_copy((me + off) % 4, me, blk, off).wait_send()
        r_copy(first, blk).wait_send()
        r_copy(second, blk).wait_send()


def fused_shards(scene_coeffs, site_ids, gripper_coeffs, order_table, wigner):
    L, NBETA, P, SL = wigner.shape
    M = SL // 2
    K = 2 * scene_coeffs.shape[1]
    BO = NBETA // 2
    NB = P // ROWS
    chosen = lax.dynamic_index_in_dim(scene_coeffs, site_ids[0], axis=4, keepdims=False)
    s = jnp.transpose(chosen, (2, 0, 1, 3)).reshape(2, L // 2, K, P)
    s = jnp.concatenate([s[0], s[1]], axis=-1)
    vmem = pl.BlockSpec(memory_space=pltpu.VMEM)
    return pl.pallas_call(
        fused_kernel,
        out_shape=jax.ShapeDtypeStruct((1, BO, P, SL), F32),
        in_specs=[vmem, vmem, vmem, pl.BlockSpec(memory_space=pl.ANY)],
        out_specs=vmem,
        scratch_shapes=[
            pltpu.VMEM((2, 2, L // 2, NBETA, P, M), BF16),
            pltpu.VMEM((4, L // 2, K, 2 * P), BF16),
            pltpu.VMEM((2, L // 2 // CHUNKS, 2 * P, M), BF16),
            pltpu.VMEM((2, NB, NBETA, 2, ROWS, M), F32),
            pltpu.VMEM((2, NB, BO, 2, ROWS, M), BF16),
            pltpu.VMEM((2, NB, BO, 2, ROWS, M), BF16),
            pltpu.VMEM((4, NB, BO * ROWS, M), BF16),
            pltpu.VMEM((4, NB, BO * ROWS, M), BF16),
            pltpu.VMEM((NB, BO * ROWS, 2 * SL), F32),
            pltpu.VMEM((2, 2 * M, 2 * SL), BF16),
            pltpu.VMEM((2, 2 * M, 2 * SL), BF16),
            pltpu.VMEM((SL, 2 * SL), BF16),
            pltpu.VMEM((SL, 2 * SL), BF16),
            pltpu.VMEM((K * L, 2 * P), F32),
            pltpu.VMEM((SL, M), jnp.int32),
            pltpu.SemaphoreType.DMA((2, CHUNKS)),
            pltpu.SemaphoreType.DMA((2, 4, CHUNKS)),
            pltpu.SemaphoreType.DMA((4, CHUNKS)),
            pltpu.SemaphoreType.DMA((2, NB)),
            pltpu.SemaphoreType.DMA((2, NB)),
            pltpu.SemaphoreType.DMA((4, NB)),
            pltpu.SemaphoreType.DMA((4, NB)),
        ],
        compiler_params=pltpu.CompilerParams(
            collective_id=0, has_side_effects=True, vmem_limit_bytes=48 * 1024 * 1024
        ),
    )(s, gripper_coeffs, order_table.reshape(2, 1, M), wigner.reshape(2, L // 2, NBETA, P, SL))


def solution(mesh):
    fits = mesh.shape["order"] == 4 and mesh.shape["degree"] == 2 and mesh.shape["site"] == 4
    shards = fused_shards if fits else general_shards
    in_specs = (
        P(None, None, "degree", "order", None),
        P("site"),
        P(None, None, "degree", "order"),
        P(),
        P("degree", None, "order", None),
    )
    out_specs = P("site", "degree", "order", None)
    return jax.shard_map(shards, mesh=mesh, in_specs=in_specs, out_specs=out_specs, check_vma=False)
```

```python
import math

import jax
import jax.numpy as jnp
from jax import lax
from jax.experimental import pallas as pl
from jax.experimental.pallas import tpu as pltpu
from jax.sharding import PartitionSpec as P


def general_shards(scene_coeffs, site_ids, gripper_coeffs, order_table, wigner):
    highest = lax.Precision.HIGHEST
    slot_count = order_table.shape[0]
    local_deg = gripper_coeffs.shape[2]
    local_ord = gripper_coeffs.shape[3]
    cand_count = scene_coeffs.shape[4]
    site_count = site_ids.shape[0]
    order_pos = lax.axis_index("order")
    degree_pos = lax.axis_index("degree")
    orders = order_table - slot_count // 2
    angles = jnp.arange(slot_count, dtype=jnp.int32)
    phase_index = jnp.mod(orders[:, None] * angles[None, :], slot_count)
    radians = phase_index.astype(jnp.float32) * (2.0 * math.pi / slot_count)
    cosine = jnp.cos(radians)
    sine_table = jnp.sin(radians)
    magnitude = jnp.abs(orders)
    resident_degrees = degree_pos * local_deg + jnp.arange(local_deg, dtype=jnp.int32)
    owned_orders = lax.dynamic_slice_in_dim(magnitude, order_pos * local_ord, local_ord)
    grip_allowed = owned_orders[None, :] <= resident_degrees[:, None]
    selector = (jnp.arange(cand_count, dtype=jnp.int32)[:, None] == site_ids[None, :]).astype(
        jnp.bfloat16
    )
    chosen = jnp.dot(
        scene_coeffs.reshape(-1, cand_count), selector, preferred_element_type=jnp.float32
    )
    chosen = chosen.astype(jnp.bfloat16).reshape(
        2, scene_coeffs.shape[1], local_deg, local_ord, site_count
    )
    grip_real = jnp.concatenate([gripper_coeffs[0], gripper_coeffs[1]], axis=0)
    grip_imag = jnp.concatenate([-gripper_coeffs[1], gripper_coeffs[0]], axis=0)
    gripper_couple = jnp.stack([grip_real, grip_imag])
    columns_in = lax.all_gather(chosen, "order", axis=3, tiled=True)
    scene_joined = jnp.concatenate([columns_in[0], columns_in[1]], axis=0)
    product = jnp.einsum(
        "aonw,iaob->iobnw", scene_joined, gripper_couple, preferred_element_type=jnp.float32
    )
    permitted_mask = grip_allowed[:, :, None] & (
        magnitude[None, None, :] <= resident_degrees[:, None, None]
    )
    product = jnp.where(permitted_mask[None, :, :, :, None], product, jnp.float32(0.0)).astype(
        jnp.bfloat16
    )
    partial_value = jnp.einsum(
        "ylprs,lbpr->ysbpr", product, wigner, preferred_element_type=jnp.float32
    )
    summed = lax.psum_scatter(partial_value, "degree", scatter_dimension=2, tiled=True)
    phase_pair = jnp.concatenate([cosine, sine_table], axis=1)
    products = jnp.einsum(
        "xsbpm,mk->xsbpk", summed, phase_pair, precision=highest, preferred_element_type=jnp.float32
    )
    real_alpha = products[0, ..., :slot_count] - products[1, ..., slot_count:]
    imag_alpha = products[0, ..., slot_count:] + products[1, ..., :slot_count]
    stacked_parts = jnp.stack([real_alpha, imag_alpha])
    exchanged = lax.all_to_all(stacked_parts, "order", split_axis=4, concat_axis=3, tiled=True)
    first_term = jnp.einsum(
        "sbpa,pk->sbak", exchanged[0], cosine, precision=highest, preferred_element_type=jnp.float32
    )
    latter_addend = jnp.einsum(
        "sbpa,pk->sbak",
        exchanged[1],
        sine_table,
        precision=highest,
        preferred_element_type=jnp.float32,
    )
    return first_term - latter_addend


MESH = pl.DeviceIdType.MESH
F32, BF16 = jnp.float32, jnp.bfloat16
CHUNKS = 4
ROWS = 16
VMEM_LIMIT = 66633728


def cos_of(index, count):
    centred = jnp.bitwise_and(index + count // 2, count - 1) - count // 2
    half = centred.astype(F32) * F32(math.pi / count)
    sq = half * half
    poly = F32(-1.0 / 39916800.0)
    for coefficient in (1.0 / 362880.0, -1.0 / 5040.0, 1.0 / 120.0, -1.0 / 6.0, 1.0):
        poly = poly * sq + F32(coefficient)
    sine = poly * half
    return 1.0 - 2.0 * sine * sine


def split(value):
    high = value.astype(BF16)
    return high, (value - high.astype(F32)).astype(BF16)


def fused_kernel(
    s_ref, g_ref, row_ref, w_ref, out_ref,
    wbuf, sbuf, prod, accbuf, rs_send, rs_recv, a_send, a_recv, halfacc,
    alpha_hi, alpha_lo, gamma_hi, gamma_lo, g32, col, g_buf, row_buf,
    in_sem, w_sem, s_send_sem, s_recv_sem, r_send_sem, r_recv_sem, x_send_sem, x_recv_sem,
):
    me = lax.axis_index("order")
    deg = lax.axis_index("degree")
    HL, NBETA, P, M = wbuf.shape[2:]
    L = 2 * HL
    SL = 2 * M
    BO = NBETA // 2
    K = s_ref.shape[1]
    first = me // 2
    second = 1 - first
    near = first * 2 + (1 - me % 2)
    per = HL // CHUNKS
    blocks = P // ROWS

    def w_copy(h, c):
        return pltpu.make_async_copy(
            w_ref.at[:, pl.ds(c * per, per), :, :, pl.ds(pl.multiple_of(h * M, M), M)],
            wbuf.at[h, :, pl.ds(c * per, per)],
            w_sem.at[h, c],
        )

    barrier = pltpu.get_barrier_semaphore()
    for off in (1, 2, 3):
        pl.semaphore_signal(barrier, 1, device_id={"order": (me + off) % 4}, device_id_type=MESH)
    pl.semaphore_signal(barrier, 1, device_id={"degree": 1 - deg}, device_id_type=MESH)

    row_copy = pltpu.make_async_copy(row_ref, row_buf, in_sem.at[0])
    g_copy = pltpu.make_async_copy(g_ref, g_buf, in_sem.at[1])
    row_copy.start()
    g_copy.start()
    for h in (first, second):
        for c in range(CHUNKS):
            w_copy(h, c).start()

    pl.semaphore_wait(barrier, 4)

    def hop(block, c, way, own=False):
        rows = pl.ds(c * per, per)
        return pltpu.make_async_remote_copy(
            src_ref=s_ref.at[rows] if own else sbuf.at[block, rows],
            dst_ref=sbuf.at[block, rows],
            send_sem=s_send_sem.at[way, block, c], recv_sem=s_recv_sem.at[block, c],
            device_id={"order": me + 1 - 2 * way}, device_id_type=MESH,
        )

    for c in range(CHUNKS):
        @pl.when(me < 3)
        def _():
            hop(me, c, 0, True).start()

        @pl.when(me > 0)
        def _():
            hop(me, c, 1, True).start()

    s_own = pltpu.make_async_copy(s_ref, sbuf.at[me], in_sem.at[2])
    s_own.start()

    row_copy.wait()
    for h in range(2):
        line = jnp.broadcast_to(row_buf[h].astype(F32), (M, M))
        col[h * M : (h + 1) * M, :] = jnp.transpose(line).astype(jnp.int32) - SL // 2
    g_copy.wait()
    real = g_buf[0].astype(F32).reshape(K // 2 * L, P)
    imag = g_buf[1].astype(F32).reshape(K // 2 * L, P)
    g32[: K // 2 * L] = jnp.concatenate([real, -imag], axis=1)
    g32[K // 2 * L :] = jnp.concatenate([imag, real], axis=1)
    accbuf[...] = jnp.zeros_like(accbuf)
    mag_p = jnp.abs(col[pl.ds(pl.multiple_of(me * P, P), P), :])
    dims = (((0,), (0,)), ((), ()))

    def tables():
        quarter = SL // 4
        lane = lax.broadcasted_iota(jnp.int32, (P, M), 1)
        for q in range(4):
            orders = col[q * P : (q + 1) * P, :]
            for t in range(4):
                at = slice(t * M, (t + 1) * M)
                phase = orders * (t * P + lane % P)
                for x in range(2):
                    hi, lo = split(cos_of(phase + (x - lane // P) * quarter, SL))
                    alpha_hi[q, x * P : (x + 1) * P, at] = hi
                    alpha_lo[q, x * P : (x + 1) * P, at] = lo
                phase = orders * ((t % 2) * M + lane)
                hi, lo = split(cos_of(phase + (t // 2) * quarter, SL))
                gamma_hi[q * P : (q + 1) * P, at] = hi
                gamma_lo[q * P : (q + 1) * P, at] = lo

    def r_copy(q, blk):
        return pltpu.make_async_remote_copy(
            src_ref=rs_send.at[q, blk], dst_ref=rs_recv.at[q, blk],
            send_sem=r_send_sem.at[q, blk], recv_sem=r_recv_sem.at[q, blk],
            device_id={"degree": 1 - deg}, device_id_type=MESH,
        )

    def packed(q, blk, who):
        held = accbuf[q // 2, blk, pl.ds(who * BO, BO)]
        upper = q % 2 == 1
        parts = [jnp.where(upper, held[:, x, :, P:], held[:, x, :, :P]) for x in range(2)]
        return jnp.concatenate(parts, axis=-1)

    def compute(h, quarters, arrivals, passing=None):
        wide = len(quarters) == 2
        only = quarters[0] % 2
        lanes = lax.broadcasted_iota(jnp.int32, (2 * P, M), 1) // P
        mag_m = jnp.abs(row_buf[h] - SL // 2)
        most = jnp.maximum(mag_p, jnp.broadcast_to(mag_m, (P, M)))
        most = jnp.concatenate([most, most], axis=0)
        if not wide:
            most = jnp.where(lanes == only, most, SL)

        def chunk(c, carry):
            arrivals(c)
            for i in range(per):
                step = c * per + i
                if wide:
                    b0, b1 = sbuf[2 * h, step], sbuf[2 * h + 1, step]
                else:
                    b0 = b1 = sbuf[quarters[0], step]
                low = jnp.concatenate([b0[:, :P], b1[:, :P]], axis=1)
                high = jnp.concatenate([b0[:, P:], b1[:, P:]], axis=1)
                for part, scene in ((0, low), (1, high)):
                    l = step + part * HL
                    grip = g32[pl.ds(l, K, stride=L), :].astype(BF16)
                    value = lax.dot_general(grip, scene, dims, preferred_element_type=F32)
                    value = jnp.where(most <= deg * L + l, value, F32(0.0))
                    prod[part, i] = value.astype(BF16)
            if passing is None or passing is arrivals_after_a:
                w_copy(h, c).wait()

            def rows(blk, carry):
                at = pl.multiple_of(blk * ROWS, ROWS)

                def degree_step(i, acc):
                    acc = list(acc)
                    for part in range(2):
                        pr = prod[part, i, pl.ds(at, ROWS), :].astype(F32)
                        pi = prod[part, i, pl.ds(at + P, ROWS), :].astype(F32)
                        for b in range(NBETA):
                            w = wbuf[h, part, c * per + i, b, pl.ds(at, ROWS), :].astype(F32)
                            acc[2 * b] += pr * w
                            acc[2 * b + 1] += pi * w
                    return tuple(acc)

                acc = tuple(accbuf[h, blk, n // 2, n % 2] for n in range(2 * NBETA))
                acc = lax.fori_loop(0, per, degree_step, acc, unroll=2)
                for n in range(2 * NBETA):
                    accbuf[h, blk, n // 2, n % 2] = acc[n]

                @pl.when(c == CHUNKS - 1)
                def _():
                    for q in quarters:
                        rs_send[q, blk] = packed(q, blk, 1 - deg).astype(BF16)
                        r_copy(q, blk).start()

                return carry

            lax.fori_loop(0, blocks, rows, 0)
            if passing is not None:
                passing(c)
            return carry

        lax.fori_loop(0, CHUNKS, chunk, 0)

    def alpha(q, blks):
        pieces = []
        for blk in blks:
            r_copy(q, blk).wait_recv()
            piece = packed(q, blk, deg) + rs_recv[q, blk].astype(F32)
            pieces.append(piece.reshape(BO * ROWS, M))
        total = pieces[0] if len(pieces) == 1 else jnp.concatenate(pieces, axis=0)
        hi, lo = split(total)
        value = jnp.dot(hi, alpha_hi[q], preferred_element_type=F32)
        value += jnp.dot(hi, alpha_lo[q], preferred_element_type=F32)
        value += jnp.dot(lo, alpha_hi[q], preferred_element_type=F32)
        return value

    across = lax.max(me - 1, 0) % 2
    middle = (me == 1) | (me == 2)
    other = me + 1 - 2 * across
    beyond = other + 1 - 2 * across

    def wait_block(block, c):
        hop(block, c, me // 3).wait_recv()

    def arrivals_first(c):
        wait_block(near, c)

        @pl.when(middle)
        def _():
            hop(near, c, across).start()
            wait_block(other, c)
            hop(other, c, 1 - across).start()

    early = jnp.where(me < 2, 2, 1)
    late = jnp.where(me < 2, 3, 0)

    def arrivals_a(c):
        @pl.when(jnp.logical_not(middle))
        def _():
            wait_block(early, c)

    def arrivals_after_a(c):
        @pl.when(middle)
        def _():
            wait_block(beyond, c)
            hop(beyond, c, 1 - across).start()

    def arrivals_b(c):
        @pl.when(jnp.logical_not(middle))
        def _():
            wait_block(late, c)

    every = tuple(range(blocks))
    tables()
    s_own.wait()
    compute(first, (first * 2, first * 2 + 1), arrivals_first)
    compute(second, (early,), arrivals_a, arrivals_after_a)
    halfacc[...] = alpha(first * 2, every) + alpha(first * 2 + 1, every)
    compute(second, (late,), arrivals_b, lambda c: None)
    halfacc[...] += alpha(early, every)

    def x_copy(target, source, blk, off):
        return pltpu.make_async_remote_copy(
            src_ref=a_send.at[target, blk], dst_ref=a_recv.at[source, blk],
            send_sem=x_send_sem.at[off, blk], recv_sem=x_recv_sem.at[off, blk],
            device_id={"order": target}, device_id_type=MESH,
        )

    for blk in range(blocks):
        mine = slice(blk * BO * ROWS, (blk + 1) * BO * ROWS)
        value = (halfacc[mine, :] + alpha(late, (blk,))).astype(BF16)
        for t in range(4):
            a_send[t, blk] = value[:, t * M : (t + 1) * M]
        for off in (2, 1, 3):
            x_copy((me + off) % 4, me, blk, off).start()
        a_recv[me, blk] = a_send[me, blk]

    for blk in range(blocks):
        for off in (1, 3, 2):
            source = (me - off + 4) % 4
            x_copy(source, source, blk, off).wait_recv()

    score = jnp.zeros((BO * P, SL), F32)
    got = [
        jnp.concatenate(
            [a_recv[z, blk, b * ROWS : (b + 1) * ROWS, :] for z in range(4) for blk in range(blocks)],
            axis=0,
        )
        for b in range(BO)
    ]
    for x in range(2):
        left = jnp.concatenate([piece[:, x * P : (x + 1) * P] for piece in got], axis=1)
        for table in (gamma_hi, gamma_lo):
            score += lax.dot_general(
                left, table[:, x * SL : (x + 1) * SL], dims, preferred_element_type=F32
            )
    out_ref[0] = score.reshape(BO, P, SL)

    for c in range(CHUNKS):
        @pl.when(me < 3)
        def _():
            hop(me, c, 0, True).wait_send()

        @pl.when(me > 0)
        def _():
            hop(me, c, 1, True).wait_send()

        @pl.when(middle)
        def _():
            hop(near, c, across).wait_send()
            hop(other, c, 1 - across).wait_send()
            hop(beyond, c, 1 - across).wait_send()

    for blk in range(blocks):
        for off in (1, 2, 3):
            x_copy((me + off) % 4, me, blk, off).wait_send()
        for q in range(4):
            r_copy(q, blk).wait_send()


def fused_shards(scene_coeffs, site_ids, gripper_coeffs, order_table, wigner):
    L, NBETA, P, SL = wigner.shape
    M = SL // 2
    K = 2 * scene_coeffs.shape[1]
    BO = NBETA // 2
    NB = P // ROWS
    chosen = lax.dynamic_index_in_dim(scene_coeffs, site_ids[0], axis=4, keepdims=False)
    s = jnp.transpose(chosen, (2, 0, 1, 3)).reshape(2, L // 2, K, P)
    s = jnp.concatenate([s[0], s[1]], axis=-1)
    vmem = pl.BlockSpec(memory_space=pltpu.VMEM)
    hbm = pl.BlockSpec(memory_space=pltpu.HBM)
    return pl.pallas_call(
        fused_kernel,
        out_shape=jax.ShapeDtypeStruct((1, BO, P, SL), F32),
        in_specs=[hbm, hbm, hbm, hbm],
        out_specs=vmem,
        scratch_shapes=[
            pltpu.VMEM((2, 2, L // 2, NBETA, P, M), BF16),
            pltpu.VMEM((4, L // 2, K, 2 * P), BF16),
            pltpu.VMEM((2, L // 2 // CHUNKS, 2 * P, M), BF16),
            pltpu.VMEM((2, NB, NBETA, 2, ROWS, M), F32),
            pltpu.VMEM((4, NB, BO, ROWS, M), BF16),
            pltpu.VMEM((4, NB, BO, ROWS, M), BF16),
            pltpu.VMEM((4, NB, BO * ROWS, M), BF16),
            pltpu.VMEM((4, NB, BO * ROWS, M), BF16),
            pltpu.VMEM((NB * BO * ROWS, 2 * SL), F32),
            pltpu.VMEM((4, M, 2 * SL), BF16),
            pltpu.VMEM((4, M, 2 * SL), BF16),
            pltpu.VMEM((SL, 2 * SL), BF16),
            pltpu.VMEM((SL, 2 * SL), BF16),
            pltpu.VMEM((K * L, 2 * P), F32),
            pltpu.VMEM((SL, M), jnp.int32),
            pltpu.VMEM((2, K // 2, L, P), BF16),
            pltpu.VMEM((2, 1, M), jnp.int32),
            pltpu.SemaphoreType.DMA((3,)),
            pltpu.SemaphoreType.DMA((2, CHUNKS)),
            pltpu.SemaphoreType.DMA((2, 4, CHUNKS)),
            pltpu.SemaphoreType.DMA((4, CHUNKS)),
            pltpu.SemaphoreType.DMA((4, NB)),
            pltpu.SemaphoreType.DMA((4, NB)),
            pltpu.SemaphoreType.DMA((4, NB)),
            pltpu.SemaphoreType.DMA((4, NB)),
        ],
        compiler_params=pltpu.CompilerParams(
            collective_id=0, has_side_effects=True, vmem_limit_bytes=VMEM_LIMIT
        ),
    )(s, gripper_coeffs, order_table.reshape(2, 1, M), wigner.reshape(2, L // 2, NBETA, P, SL))


def solution(mesh):
    fits = mesh.shape["order"] == 4 and mesh.shape["degree"] == 2 and mesh.shape["site"] == 4
    shards = fused_shards if fits else general_shards
    in_specs = (
        P(None, None, "degree", "order", None),
        P("site"),
        P(None, None, "degree", "order"),
        P(),
        P("degree", None, "order", None),
    )
    out_specs = P("site", "degree", "order", None)
    return jax.shard_map(shards, mesh=mesh, in_specs=in_specs, out_specs=out_specs, check_vma=False)
```

```python
import math

import jax
import jax.numpy as jnp
from jax import lax
from jax.experimental import pallas as pl
from jax.experimental.pallas import tpu as pltpu
from jax.sharding import PartitionSpec as P


def general_shards(scene_coeffs, site_ids, gripper_coeffs, order_table, wigner):
    highest = lax.Precision.HIGHEST
    slot_count = order_table.shape[0]
    local_deg = gripper_coeffs.shape[2]
    local_ord = gripper_coeffs.shape[3]
    cand_count = scene_coeffs.shape[4]
    site_count = site_ids.shape[0]
    order_pos = lax.axis_index("order")
    degree_pos = lax.axis_index("degree")
    orders = order_table - slot_count // 2
    angles = jnp.arange(slot_count, dtype=jnp.int32)
    phase_index = jnp.mod(orders[:, None] * angles[None, :], slot_count)
    radians = phase_index.astype(jnp.float32) * (2.0 * math.pi / slot_count)
    cosine = jnp.cos(radians)
    sine_table = jnp.sin(radians)
    magnitude = jnp.abs(orders)
    resident_degrees = degree_pos * local_deg + jnp.arange(local_deg, dtype=jnp.int32)
    owned_orders = lax.dynamic_slice_in_dim(magnitude, order_pos * local_ord, local_ord)
    grip_allowed = owned_orders[None, :] <= resident_degrees[:, None]
    selector = (jnp.arange(cand_count, dtype=jnp.int32)[:, None] == site_ids[None, :]).astype(
        jnp.bfloat16
    )
    chosen = jnp.dot(
        scene_coeffs.reshape(-1, cand_count), selector, preferred_element_type=jnp.float32
    )
    chosen = chosen.astype(jnp.bfloat16).reshape(
        2, scene_coeffs.shape[1], local_deg, local_ord, site_count
    )
    grip_real = jnp.concatenate([gripper_coeffs[0], gripper_coeffs[1]], axis=0)
    grip_imag = jnp.concatenate([-gripper_coeffs[1], gripper_coeffs[0]], axis=0)
    gripper_couple = jnp.stack([grip_real, grip_imag])
    columns_in = lax.all_gather(chosen, "order", axis=3, tiled=True)
    scene_joined = jnp.concatenate([columns_in[0], columns_in[1]], axis=0)
    product = jnp.einsum(
        "aonw,iaob->iobnw", scene_joined, gripper_couple, preferred_element_type=jnp.float32
    )
    permitted_mask = grip_allowed[:, :, None] & (
        magnitude[None, None, :] <= resident_degrees[:, None, None]
    )
    product = jnp.where(permitted_mask[None, :, :, :, None], product, jnp.float32(0.0)).astype(
        jnp.bfloat16
    )
    partial_value = jnp.einsum(
        "ylprs,lbpr->ysbpr", product, wigner, preferred_element_type=jnp.float32
    )
    summed = lax.psum_scatter(partial_value, "degree", scatter_dimension=2, tiled=True)
    phase_pair = jnp.concatenate([cosine, sine_table], axis=1)
    products = jnp.einsum(
        "xsbpm,mk->xsbpk", summed, phase_pair, precision=highest, preferred_element_type=jnp.float32
    )
    real_alpha = products[0, ..., :slot_count] - products[1, ..., slot_count:]
    imag_alpha = products[0, ..., slot_count:] + products[1, ..., :slot_count]
    stacked_parts = jnp.stack([real_alpha, imag_alpha])
    exchanged = lax.all_to_all(stacked_parts, "order", split_axis=4, concat_axis=3, tiled=True)
    first_term = jnp.einsum(
        "sbpa,pk->sbak", exchanged[0], cosine, precision=highest, preferred_element_type=jnp.float32
    )
    latter_addend = jnp.einsum(
        "sbpa,pk->sbak",
        exchanged[1],
        sine_table,
        precision=highest,
        preferred_element_type=jnp.float32,
    )
    return first_term - latter_addend


MESH = pl.DeviceIdType.MESH
F32, BF16 = jnp.float32, jnp.bfloat16
CHUNKS = 8
ROWS = 16


def cos_of(index, count):
    centred = jnp.bitwise_and(index + count // 2, count - 1) - count // 2
    half = centred.astype(F32) * F32(math.pi / count)
    sq = half * half
    poly = F32(-1.0 / 39916800.0)
    for coefficient in (1.0 / 362880.0, -1.0 / 5040.0, 1.0 / 120.0, -1.0 / 6.0, 1.0):
        poly = poly * sq + F32(coefficient)
    sine = poly * half
    return 1.0 - 2.0 * sine * sine


def split(value):
    high = value.astype(BF16)
    return high, (value - high.astype(F32)).astype(BF16)


def fused_kernel(
    s_ref, g_ref, row_ref, w_ref, out_ref,
    wbuf, sbuf, prod, accbuf, rs_send, rs_recv, a_send, a_recv, halfacc,
    alpha_hi, alpha_lo, gamma_hi, gamma_lo, g32, col,
    w_sem, s_send_sem, s_recv_sem, r_send_sem, r_recv_sem, x_send_sem, x_recv_sem,
):
    me = lax.axis_index("order")
    deg = lax.axis_index("degree")
    HL, NBETA, P, M = wbuf.shape[2:]
    L = 2 * HL
    SL = 2 * M
    BO = NBETA // 2
    K = s_ref.shape[1]
    first = me // 2
    second = 1 - first
    near = first * 2 + (1 - me % 2)
    per = HL // CHUNKS
    blocks = P // ROWS

    def w_copy(h, c):
        return pltpu.make_async_copy(
            w_ref.at[:, pl.ds(c * per, per), :, :, pl.ds(pl.multiple_of(h * M, M), M)],
            wbuf.at[h, :, pl.ds(c * per, per)],
            w_sem.at[h, c],
        )

    barrier = pltpu.get_barrier_semaphore()
    for off in (1, 2, 3):
        pl.semaphore_signal(barrier, 1, device_id={"order": (me + off) % 4}, device_id_type=MESH)
    pl.semaphore_signal(barrier, 1, device_id={"degree": 1 - deg}, device_id_type=MESH)

    for h in (first, second):
        for c in range(CHUNKS):
            w_copy(h, c).start()

    pl.semaphore_wait(barrier, 4)

    def hop(block, c, way, own=False):
        rows = pl.ds(c * per, per)
        return pltpu.make_async_remote_copy(
            src_ref=s_ref.at[rows] if own else sbuf.at[block, rows],
            dst_ref=sbuf.at[block, rows],
            send_sem=s_send_sem.at[way, block, c], recv_sem=s_recv_sem.at[block, c],
            device_id={"order": me + 1 - 2 * way}, device_id_type=MESH,
        )

    for c in range(CHUNKS):
        @pl.when(me < 3)
        def _():
            hop(me, c, 0, True).start()

        @pl.when(me > 0)
        def _():
            hop(me, c, 1, True).start()

    sbuf[me] = s_ref[...]

    for h in range(2):
        line = jnp.broadcast_to(row_ref[h].astype(F32), (M, M))
        col[h * M : (h + 1) * M, :] = jnp.transpose(line).astype(jnp.int32) - SL // 2
    real = g_ref[0].astype(F32).reshape(K // 2 * L, P)
    imag = g_ref[1].astype(F32).reshape(K // 2 * L, P)
    g32[: K // 2 * L] = jnp.concatenate([real, -imag], axis=1)
    g32[K // 2 * L :] = jnp.concatenate([imag, real], axis=1)
    accbuf[...] = jnp.zeros_like(accbuf)
    mag_p = jnp.abs(col[pl.ds(pl.multiple_of(me * P, P), P), :])
    dims = (((0,), (0,)), ((), ()))

    def tables():
        quarter = SL // 4
        lane = lax.broadcasted_iota(jnp.int32, (M, M), 1)
        for h in range(2):
            orders = col[h * M : (h + 1) * M, :]
            for t in range(4):
                at = slice(t * M, (t + 1) * M)
                phase = orders * (t * P + lane % P)
                for x in range(2):
                    hi, lo = split(cos_of(phase + (x - lane // P) * quarter, SL))
                    alpha_hi[h, x * M : (x + 1) * M, at] = hi
                    alpha_lo[h, x * M : (x + 1) * M, at] = lo
                phase = orders * ((t % 2) * M + lane)
                hi, lo = split(cos_of(phase + (t // 2) * quarter, SL))
                gamma_hi[h * M : (h + 1) * M, at] = hi
                gamma_lo[h * M : (h + 1) * M, at] = lo

    def r_copy(h, blk):
        return pltpu.make_async_remote_copy(
            src_ref=rs_send.at[h, blk], dst_ref=rs_recv.at[h, blk],
            send_sem=r_send_sem.at[h, blk], recv_sem=r_recv_sem.at[h, blk],
            device_id={"degree": 1 - deg}, device_id_type=MESH,
        )

    def compute(h, arrivals):
        mag_m = jnp.abs(row_ref[h] - SL // 2)
        most = jnp.maximum(mag_p, jnp.broadcast_to(mag_m, (P, M)))
        most = jnp.concatenate([most, most], axis=0)

        def chunk(c, carry):
            arrivals(c)
            for i in range(per):
                step = c * per + i
                b0, b1 = sbuf[2 * h, step], sbuf[2 * h + 1, step]
                low = jnp.concatenate([b0[:, :P], b1[:, :P]], axis=1)
                high = jnp.concatenate([b0[:, P:], b1[:, P:]], axis=1)
                for part, scene in ((0, low), (1, high)):
                    l = step + part * HL
                    grip = g32[pl.ds(l, K, stride=L), :].astype(BF16)
                    value = lax.dot_general(grip, scene, dims, preferred_element_type=F32)
                    value = jnp.where(most <= deg * L + l, value, F32(0.0))
                    prod[part, i] = value.astype(BF16)
            w_copy(h, c).wait()

            def rows(blk, carry):
                at = pl.multiple_of(blk * ROWS, ROWS)

                def degree_step(i, acc):
                    acc = list(acc)
                    for part in range(2):
                        pr = prod[part, i, pl.ds(at, ROWS), :].astype(F32)
                        pi = prod[part, i, pl.ds(at + P, ROWS), :].astype(F32)
                        for b in range(NBETA):
                            w = wbuf[h, part, c * per + i, b, pl.ds(at, ROWS), :].astype(F32)
                            acc[2 * b] += pr * w
                            acc[2 * b + 1] += pi * w
                    return tuple(acc)

                acc = tuple(accbuf[h, blk, n // 2, n % 2] for n in range(2 * NBETA))
                acc = lax.fori_loop(0, per, degree_step, acc, unroll=2)
                for n in range(2 * NBETA):
                    accbuf[h, blk, n // 2, n % 2] = acc[n]

                @pl.when(c == CHUNKS - 1)
                def _():
                    rs_send[h, blk] = accbuf[h, blk, pl.ds((1 - deg) * BO, BO)].astype(BF16)
                    r_copy(h, blk).start()

                return carry

            return lax.fori_loop(0, blocks, rows, carry)

        lax.fori_loop(0, CHUNKS, chunk, 0)

    def alpha(h, blk):
        r_copy(h, blk).wait_recv()
        total = accbuf[h, blk, pl.ds(deg * BO, BO)] + rs_recv[h, blk].astype(F32)
        total = jnp.concatenate(
            [total[:, 0].reshape(BO * ROWS, M), total[:, 1].reshape(BO * ROWS, M)], axis=1
        )
        hi, lo = split(total)
        value = jnp.dot(hi, alpha_hi[h], preferred_element_type=F32)
        value += jnp.dot(hi, alpha_lo[h], preferred_element_type=F32)
        value += jnp.dot(lo, alpha_hi[h], preferred_element_type=F32)
        return value

    across = lax.max(me - 1, 0) % 2
    middle = (me == 1) | (me == 2)
    other = me + 1 - 2 * across
    beyond = other + 1 - 2 * across

    def wait_block(block, c):
        hop(block, c, me // 3).wait_recv()

    def arrivals_first(c):
        wait_block(near, c)

        @pl.when(middle)
        def _():
            hop(near, c, across).start()
            wait_block(other, c)
            hop(other, c, 1 - across).start()

    def arrivals_second(c):
        @pl.when(middle)
        def _():
            wait_block(beyond, c)
            hop(beyond, c, 1 - across).start()

        @pl.when(jnp.logical_not(middle))
        def _():
            wait_block(second * 2, c)
            wait_block(second * 2 + 1, c)

    tables()
    compute(first, arrivals_first)
    compute(second, arrivals_second)

    def x_copy(target, source, blk, off):
        return pltpu.make_async_remote_copy(
            src_ref=a_send.at[target, blk], dst_ref=a_recv.at[source, blk],
            send_sem=x_send_sem.at[off, blk], recv_sem=x_recv_sem.at[off, blk],
            device_id={"order": target}, device_id_type=MESH,
        )

    for blk in range(blocks):
        halfacc[blk] = alpha(first, blk)
    for blk in range(blocks):
        value = (halfacc[blk] + alpha(second, blk)).astype(BF16)
        for t in range(4):
            a_send[t, blk] = value[:, t * M : (t + 1) * M]
        for off in (2, 1, 3):
            x_copy((me + off) % 4, me, blk, off).start()
        a_recv[me, blk] = a_send[me, blk]

    for blk in range(blocks):
        for off in (1, 3, 2):
            source = (me - off + 4) % 4
            x_copy(source, source, blk, off).wait_recv()

    score = jnp.zeros((BO * P, SL), F32)
    got = [
        jnp.concatenate(
            [a_recv[z, blk, b * ROWS : (b + 1) * ROWS, :] for z in range(4) for blk in range(blocks)],
            axis=0,
        )
        for b in range(BO)
    ]
    for x in range(2):
        left = jnp.concatenate([piece[:, x * P : (x + 1) * P] for piece in got], axis=1)
        for table in (gamma_hi, gamma_lo):
            score += lax.dot_general(
                left, table[:, x * SL : (x + 1) * SL], dims, preferred_element_type=F32
            )
    out_ref[0] = score.reshape(BO, P, SL)

    for c in range(CHUNKS):
        @pl.when(me < 3)
        def _():
            hop(me, c, 0, True).wait_send()

        @pl.when(me > 0)
        def _():
            hop(me, c, 1, True).wait_send()

        @pl.when(middle)
        def _():
            hop(near, c, across).wait_send()
            hop(other, c, 1 - across).wait_send()
            hop(beyond, c, 1 - across).wait_send()

    for blk in range(blocks):
        for off in (1, 2, 3):
            x_copy((me + off) % 4, me, blk, off).wait_send()
        r_copy(first, blk).wait_send()
        r_copy(second, blk).wait_send()


def fused_shards(scene_coeffs, site_ids, gripper_coeffs, order_table, wigner):
    L, NBETA, P, SL = wigner.shape
    M = SL // 2
    K = 2 * scene_coeffs.shape[1]
    BO = NBETA // 2
    NB = P // ROWS
    chosen = lax.dynamic_index_in_dim(scene_coeffs, site_ids[0], axis=4, keepdims=False)
    s = jnp.transpose(chosen, (2, 0, 1, 3)).reshape(2, L // 2, K, P)
    s = jnp.concatenate([s[0], s[1]], axis=-1)
    vmem = pl.BlockSpec(memory_space=pltpu.VMEM)
    return pl.pallas_call(
        fused_kernel,
        out_shape=jax.ShapeDtypeStruct((1, BO, P, SL), F32),
        in_specs=[vmem, vmem, vmem, pl.BlockSpec(memory_space=pl.ANY)],
        out_specs=vmem,
        scratch_shapes=[
            pltpu.VMEM((2, 2, L // 2, NBETA, P, M), BF16),
            pltpu.VMEM((4, L // 2, K, 2 * P), BF16),
            pltpu.VMEM((2, L // 2 // CHUNKS, 2 * P, M), BF16),
            pltpu.VMEM((2, NB, NBETA, 2, ROWS, M), F32),
            pltpu.VMEM((2, NB, BO, 2, ROWS, M), BF16),
            pltpu.VMEM((2, NB, BO, 2, ROWS, M), BF16),
            pltpu.VMEM((4, NB, BO * ROWS, M), BF16),
            pltpu.VMEM((4, NB, BO * ROWS, M), BF16),
            pltpu.VMEM((NB, BO * ROWS, 2 * SL), F32),
            pltpu.VMEM((2, 2 * M, 2 * SL), BF16),
            pltpu.VMEM((2, 2 * M, 2 * SL), BF16),
            pltpu.VMEM((SL, 2 * SL), BF16),
            pltpu.VMEM((SL, 2 * SL), BF16),
            pltpu.VMEM((K * L, 2 * P), F32),
            pltpu.VMEM((SL, M), jnp.int32),
            pltpu.SemaphoreType.DMA((2, CHUNKS)),
            pltpu.SemaphoreType.DMA((2, 4, CHUNKS)),
            pltpu.SemaphoreType.DMA((4, CHUNKS)),
            pltpu.SemaphoreType.DMA((2, NB)),
            pltpu.SemaphoreType.DMA((2, NB)),
            pltpu.SemaphoreType.DMA((4, NB)),
            pltpu.SemaphoreType.DMA((4, NB)),
        ],
        compiler_params=pltpu.CompilerParams(
            collective_id=0, has_side_effects=True, vmem_limit_bytes=48 * 1024 * 1024
        ),
    )(s, gripper_coeffs, order_table.reshape(2, 1, M), wigner.reshape(2, L // 2, NBETA, P, SL))


def solution(mesh):
    fits = mesh.shape["order"] == 4 and mesh.shape["degree"] == 2 and mesh.shape["site"] == 4
    shards = fused_shards if fits else general_shards
    in_specs = (
        P(None, None, "degree", "order", None),
        P("site"),
        P(None, None, "degree", "order"),
        P(),
        P("degree", None, "order", None),
    )
    out_specs = P("site", "degree", "order", None)
    return jax.shard_map(shards, mesh=mesh, in_specs=in_specs, out_specs=out_specs, check_vma=False)
```
